512 devices in a mesh: wide: 64 (over x, y, z_hi), grp: 8 (over z_lo, core).
Axes of the slice: x: 4, y: 4, z: 16 (z_hi: 4, z_lo: 4; z = z_hi * 4 + z_lo), core: 2. Of those that a mesh axis runs over, the one named last changes fastest.
Arguments:
- samples: bfloat16 [2048, 512], P(('wide', 'grp')), may hold values from -6 to 6
- archive: bfloat16 [262144, 512], P(('wide', 'grp')), may hold values from -6 to 6
- inv_len: float32 [512], replicated, may hold values from 0.7 to 2.8
- mean_coef: bfloat16 [262144, 64], P(('wide', 'grp')), may hold values from -0.1875 to 0.1875
- var_coef: bfloat16 [262144, 64], P(('wide', 'grp')), may hold values from -1 to 1
Outputs:
- pred_mean: float32 [2048, 64], P(('wide', 'grp'))
- pred_var: float32 [2048, 64], P(('wide', 'grp'))
The draws below stay inside these ranges and needn't reach their ends.
All inputs are finite; a program needn't handle non-finite values.
Results may differ from the reference program's by a relative error of at most 0.0085.
Values may be sent and summed in bfloat16 or wider, within the bound.
A program may use at most 64 MiB of HBM per device.

```python
import math
import jax
import jax.numpy as jnp
from jax import lax

DIN = 512
OUT = 64
M_DEV = 512
S = 2048
M_ALL = 262144


def block_scale(key, extent, cuts, low, top_value):
    def one(position, blocks):
        heights = jax.random.uniform(jax.random.fold_in(jax.random.fold_in(key, 6), position), (blocks,), jnp.float32, low / len(cuts), top_value / len(cuts))
        return jnp.repeat(jnp.exp(heights), extent[position] // blocks).reshape((-1,) + (1,) * (len(extent) - position - 1))

    gain = one(*cuts[0])
    for cut in cuts[1:]:
        gain = gain * one(*cut)
    return gain


def noise(rng, shape, deviation, reach, shards=(), held_as=jnp.bfloat16):
    array = jax.random.normal(rng, shape, jnp.float32) * deviation
    if len(shards) > 0:
        array = block_scale(rng, shape, shards, -0.22, 0.18) * array
    return jnp.clip(array, min=-reach, max=reach).astype(held_as)


def setup_inputs(seed: int = 0) -> dict:
    streams_of = jax.random.split(jax.random.key(seed), 6)
    return {
        "samples": noise(streams_of[0], (S, DIN), 1.0, 6.0, ((0, 512),)),
        "archive": noise(streams_of[1], (M_ALL, DIN), 1.0, 6.0, ((0, 512),)),
        "inv_len": jnp.clip(jnp.exp(jax.random.uniform(streams_of[2], (DIN,), jnp.float32, math.log(0.7), math.log(2.8))), 0.7, 2.8),
        "mean_coef": noise(streams_of[3], (M_ALL, OUT), (M_ALL // 256) ** -0.5, 0.1875, ((0, 512),)),
        "var_coef": noise(streams_of[4], (M_ALL, OUT), (max(1, M_ALL // 8192)) ** -0.5, 1.0, ((0, 512),)),
    }


def scaled_rows(rows, inv_len):
    factor = inv_len * (DIN ** -0.5)
    scaled = (rows.astype(jnp.float32) * factor).astype(jnp.bfloat16)
    wide_copy = scaled.astype(jnp.float32)
    return scaled, jnp.sum(wide_copy * wide_copy, axis=-1)


def reference(samples, archive, inv_len, mean_coef, var_coef):
    samp_z, samp_norm = scaled_rows(samples, inv_len)
    block_rows = 8 * M_DEV
    block_count = M_ALL // block_rows
    arch_blocks = archive.reshape(block_count, block_rows, DIN)
    mean_blocks = mean_coef.reshape(block_count, block_rows, OUT)
    var_blocks = var_coef.reshape(block_count, block_rows, OUT)

    def accumulate(totals, pieces):
        mean_sum, corr_sum = totals
        arch_rows, mean_rows, var_rows = pieces
        arch_z, arch_norm = scaled_rows(arch_rows, inv_len)
        inner_prod = jnp.dot(samp_z, arch_z.T, preferred_element_type=jnp.float32)
        kernel = jnp.exp(inner_prod - 0.5 * samp_norm[:, None] - 0.5 * arch_norm[None, :])
        kernel_half = kernel.astype(jnp.bfloat16)
        square_half = (kernel * kernel).astype(jnp.bfloat16)
        mean_sum = mean_sum + jnp.dot(kernel_half, mean_rows, preferred_element_type=jnp.float32)
        corr_sum = corr_sum + jnp.dot(square_half, var_rows, preferred_element_type=jnp.float32)
        return (mean_sum, corr_sum), None

    start_pair = (jnp.zeros((S, OUT), jnp.float32), jnp.zeros((S, OUT), jnp.float32))
    final_pair, unused = lax.scan(accumulate, start_pair, (arch_blocks, mean_blocks, var_blocks))
    pred_mean, correction = final_pair
    return pred_mean, 1.0 - correction
```

```python
import functools

import jax
import jax.numpy as jnp
from jax import lax
from jax.experimental import pallas as pl
from jax.experimental.pallas import tpu as pltpu
from jax.sharding import PartitionSpec as P

MESH = pl.DeviceIdType.MESH
F32 = jnp.float32
BF16 = jnp.bfloat16
DIN = 512
OUT = 64
ROWS = 4
RUNS = 512
NX, NY, NZ, NC = 4, 4, 16, 2
Z_SLOTS = (0, 1, -1, 2, -2, 3, -3, 4, -4, 5, -5, 6, -6, 7, -7, 8)
GROUPS = 4
PER_GROUP = NZ // GROUPS
GROUP_ROWS = PER_GROUP * ROWS
XY = NX * NY
NT = (((1,), (1,)), ((), ()))


def slot_of(offset):
    return Z_SLOTS.index(offset if offset != -8 else 8)


def device_at(dx, dy, dz, dc):
    wide = lax.axis_index("wide")
    grp = lax.axis_index("grp")
    x = (wide // 16 + dx) % NX
    y = ((wide // 4) % 4 + dy) % NY
    z = ((wide % 4) * 4 + grp // 2 + dz) % NZ
    core = (grp % 2 + dc) % NC
    return (x * 16 + y * 4 + z // 4, (z % 4) * 2 + core)


def remote(src, dst, send_sem, recv_sem, where):
    return pltpu.make_async_remote_copy(
        src_ref=src,
        dst_ref=dst,
        send_sem=send_sem,
        recv_sem=recv_sem,
        device_id=device_at(*where),
        device_id_type=MESH,
    )


def kernel(
    samples_hbm,
    archive_hbm,
    inv_hbm,
    mean_hbm,
    var_hbm,
    out_ref,
    own_raw,
    arch_raw,
    inv,
    coef,
    arch,
    arch_half,
    z_in,
    z_wide,
    main,
    part,
    part_own,
    xy_in,
    z_out,
    z_back,
    load_sem,
    swap_send,
    swap_recv,
    z_send,
    z_recv,
    one_send,
    one_recv,
    two_send,
    two_recv,
    xy_send,
    xy_recv,
    back_send,
    back_recv,
):
    z_partners = [(0, 0, d, 0) for d in Z_SLOTS[1:]]
    xy_partners = [(a, b, 0, 0) for a in range(NX) for b in range(NY) if a or b]
    partners = z_partners + xy_partners + [(0, 0, 0, 1)]
    barrier = pltpu.get_barrier_semaphore()
    for where in partners:
        pl.semaphore_signal(barrier, inc=1, device_id=device_at(*where), device_id_type=MESH)

    loads = [
        pltpu.make_async_copy(samples_hbm, own_raw, load_sem.at[0]),
        pltpu.make_async_copy(inv_hbm, inv, load_sem.at[1]),
        pltpu.make_async_copy(archive_hbm, arch_raw, load_sem.at[2]),
        pltpu.make_async_copy(mean_hbm, coef.at[0, pl.ds(0, OUT), pl.ds(0, RUNS)], load_sem.at[3]),
        pltpu.make_async_copy(var_hbm, coef.at[1, pl.ds(OUT, OUT), pl.ds(0, RUNS)], load_sem.at[4]),
    ]
    for load in loads:
        load.start()
    coef[0, OUT : 2 * OUT, :] = jnp.zeros((OUT, 2 * RUNS), BF16)
    coef[1, 0:OUT, :] = jnp.zeros((OUT, 2 * RUNS), BF16)
    loads[0].wait()
    loads[1].wait()
    factor = inv[...] * DIN ** (-0.5)
    z_in[0] = (own_raw[...].astype(F32) * factor).astype(BF16)
    loads[2].wait()
    scaled = (arch_raw[...].astype(F32) * factor).astype(BF16)
    arch[0:RUNS, :] = scaled
    wide_copy = scaled.astype(F32)
    half_norm = 0.5 * jnp.sum(wide_copy * wide_copy, axis=-1, keepdims=True)
    arch_half[:, 0:RUNS] = jnp.transpose(jnp.broadcast_to(half_norm, (RUNS, 128)))[0:8, :]
    loads[3].wait()
    loads[4].wait()

    pl.semaphore_wait(barrier, len(partners))

    for slot in range(NZ - 1, 0, -1):
        there = slot_of(-Z_SLOTS[slot])
        remote(
            z_in.at[0], z_in.at[there], z_send.at[0], z_recv.at[there // PER_GROUP], (0, 0, Z_SLOTS[slot], 0)
        ).start()
    here, other = pl.ds(0, RUNS), pl.ds(RUNS, RUNS)
    low, high = pl.ds(0, OUT), pl.ds(OUT, OUT)
    swap = [
        remote(arch.at[here], arch.at[other], swap_send.at[0], swap_recv.at[0], (0, 0, 0, 1)),
        remote(arch_half.at[:, here], arch_half.at[:, other], swap_send.at[1], swap_recv.at[1], (0, 0, 0, 1)),
        remote(coef.at[0, low, here], coef.at[0, low, other], swap_send.at[2], swap_recv.at[2], (0, 0, 0, 1)),
        remote(coef.at[1, high, here], coef.at[1, high, other], swap_send.at[3], swap_recv.at[3], (0, 0, 0, 1)),
    ]
    for copy in swap:
        copy.start()

    rest = pl.ds(1, 3)

    def y_first(group):
        return group % 2 == 0

    def from_z(group):
        first = max(1, group * PER_GROUP)
        landed = z_in.at[pl.ds(first, (group + 1) * PER_GROUP - first)]
        remote(landed, landed, z_send.at[0], z_recv.at[group], (0, 0, 1, 0)).wait_recv()
        for place in range(PER_GROUP):
            z_wide[place * ROWS : (place + 1) * ROWS, :] = z_in[group * PER_GROUP + place].astype(F32)
        main[group, 0, 0] = z_wide[...].astype(BF16)
        for step in (1, 2, 3):
            back = 4 - step
            target = main.at[group, 0, back] if y_first(group) else main.at[group, back, 0]
            where = (0, step, 0, 0) if y_first(group) else (step, 0, 0, 0)
            remote(main.at[group, 0, 0], target, one_send.at[group], one_recv.at[group], where).start()

    def landed_one(group):
        return main.at[group, 0, rest] if y_first(group) else main.at[group, rest, 0]

    def landed_two(group):
        return main.at[group, rest] if y_first(group) else main.at[group, :, rest]

    def second(group):
        landed = landed_one(group)
        remote(landed, landed, one_send.at[group], one_recv.at[group], (1, 0, 0, 0)).wait_recv()
        for step in (1, 2, 3):
            back = 4 - step
            source = main.at[group, 0] if y_first(group) else main.at[group, :, 0]
            target = main.at[group, back] if y_first(group) else main.at[group, :, back]
            where = (step, 0, 0, 0) if y_first(group) else (0, step, 0, 0)
            remote(source, target, two_send.at[group], two_recv.at[group], where).start()

    def compute(group):
        landed = landed_two(group)
        remote(landed, landed, two_send.at[group], two_recv.at[group], (1, 0, 0, 0)).wait_recv()
        block = main[group].reshape(XY * GROUP_ROWS, DIN)
        wide_block = block.astype(F32)
        samp_half = 0.5 * jnp.sum(wide_block * wide_block, axis=-1, keepdims=True)
        inner = lax.dot_general(block, arch[...], NT, preferred_element_type=F32)
        value = jnp.exp(inner - samp_half - arch_half[0:1, :])
        total = lax.dot_general(value.astype(BF16), coef[0], NT, preferred_element_type=F32)
        total = total + lax.dot_general((value * value).astype(BF16), coef[1], NT, preferred_element_type=F32)
        part_own[group] = total[0:GROUP_ROWS, :]
        part[group] = total.astype(BF16).reshape(XY, GROUP_ROWS, 2 * OUT)
        for spot in range(1, XY):
            a, b = spot // NY, spot % NY
            there = ((NX - a) % NX) * NY + (NY - b) % NY
            remote(
                part.at[group, spot], xy_in.at[group, there], xy_send.at[group], xy_recv.at[group], (a, b, 0, 0)
            ).start()

    def reduce_xy(group):
        landed = xy_in.at[group, pl.ds(1, XY - 1)]
        remote(landed, landed, xy_send.at[group], xy_recv.at[group], (1, 0, 0, 0)).wait_recv()
        total = part_own[group] + jnp.sum(xy_in[group, 1:XY].astype(F32), axis=0)
        for place in range(PER_GROUP):
            slot = group * PER_GROUP + place
            z_out[slot] = total[place * ROWS : (place + 1) * ROWS, :]
            if slot:
                there = slot_of(-Z_SLOTS[slot])
                remote(
                    z_out.at[slot], z_back.at[there], back_send.at[0], back_recv.at[0], (0, 0, Z_SLOTS[slot], 0)
                ).start()

    from_z(0)
    from_z(1)
    from_z(2)
    second(0)
    from_z(3)
    second(1)
    second(2)
    for copy in swap:
        copy.wait_recv()
    compute(0)
    second(3)
    compute(1)
    compute(2)
    compute(3)
    for group in range(GROUPS):
        reduce_xy(group)

    landed = z_back.at[pl.ds(1, NZ - 1)]
    remote(landed, landed, back_send.at[0], back_recv.at[0], (0, 0, 1, 0)).wait_recv()
    out_ref[...] = z_out[0] + jnp.sum(z_back[1:NZ], axis=0)

    sent = z_in.at[pl.ds(1, NZ - 1)]
    remote(sent, sent, z_send.at[0], z_recv.at[0], (0, 0, 1, 0)).wait_send()
    for copy in swap:
        copy.wait_send()
    for group in range(GROUPS):
        one, two, three = landed_one(group), landed_two(group), xy_in.at[group, pl.ds(1, XY - 1)]
        remote(one, one, one_send.at[group], one_recv.at[group], (1, 0, 0, 0)).wait_send()
        remote(two, two, two_send.at[group], two_recv.at[group], (1, 0, 0, 0)).wait_send()
        remote(three, three, xy_send.at[group], xy_recv.at[group], (1, 0, 0, 0)).wait_send()
    remote(landed, landed, back_send.at[0], back_recv.at[0], (0, 0, 1, 0)).wait_send()


def on_device(samples, archive, inv_len, mean_coef, var_coef):
    dma = pltpu.SemaphoreType.DMA
    sums = pl.pallas_call(
        kernel,
        out_shape=jax.ShapeDtypeStruct((ROWS, 2 * OUT), F32),
        in_specs=[pl.BlockSpec(memory_space=pl.ANY)] * 5,
        out_specs=pl.BlockSpec(memory_space=pltpu.VMEM),
        scratch_shapes=[
            pltpu.VMEM((ROWS, DIN), BF16),
            pltpu.VMEM((RUNS, DIN), BF16),
            pltpu.VMEM((1, DIN), F32),
            pltpu.VMEM((2, 2 * OUT, 2 * RUNS), BF16),
            pltpu.VMEM((2 * RUNS, DIN), BF16),
            pltpu.VMEM((8, 2 * RUNS), F32),
            pltpu.VMEM((NZ, ROWS, DIN), BF16),
            pltpu.VMEM((GROUP_ROWS, DIN), F32),
            pltpu.VMEM((GROUPS, NX, NY, GROUP_ROWS, DIN), BF16),
            pltpu.VMEM((GROUPS, XY, GROUP_ROWS, 2 * OUT), BF16),
            pltpu.VMEM((GROUPS, GROUP_ROWS, 2 * OUT), F32),
            pltpu.VMEM((GROUPS, XY, GROUP_ROWS, 2 * OUT), BF16),
            pltpu.VMEM((NZ, ROWS, 2 * OUT), F32),
            pltpu.VMEM((NZ, ROWS, 2 * OUT), F32),
            dma((5,)),
            dma((4,)),
            dma((4,)),
            dma((1,)),
            dma((GROUPS,)),
            dma((GROUPS,)),
            dma((GROUPS,)),
            dma((GROUPS,)),
            dma((GROUPS,)),
            dma((GROUPS,)),
            dma((GROUPS,)),
            dma((1,)),
            dma((1,)),
        ],
        name="surrogate",
        compiler_params=pltpu.CompilerParams(
            collective_id=0, has_side_effects=True, vmem_limit_bytes=60 << 20
        ),
    )(samples, archive, inv_len.reshape(1, DIN), mean_coef.T, var_coef.T)
    return (sums[:, :OUT], 1.0 - sums[:, OUT:])


def solution(mesh):
    rows = P(("wide", "grp"), None)
    return jax.shard_map(
        on_device,
        mesh=mesh,
        in_specs=(rows, rows, P(), rows, rows),
        out_specs=(rows, rows),
        check_vma=False,
    )
```

```python
import functools

import jax
import jax.numpy as jnp
from jax import lax
from jax.experimental import pallas as pl
from jax.experimental.pallas import tpu as pltpu
from jax.sharding import PartitionSpec as P

MESH = pl.DeviceIdType.MESH
F32 = jnp.float32
BF16 = jnp.bfloat16
DIN = 512
OUT = 64
ROWS = 4
RUNS = 512
NX, NY, NZ, NC = 4, 4, 16, 2
Z_SLOTS = (0, 1, 2, 3, 4, -1, -2, -3, -4, 5, 6, 7, 8, -5, -6, -7)
NEAR = (4, -4, 3, -3, 2, -2, 1, -1)
GROUPS = 4
DIRECT = (2, 3)
FAR_STEPS = (
    (2, 2), (2, 1), (2, 3), (1, 2), (3, 2), (2, 0), (0, 2), (1, 1),
    (1, 3), (3, 1), (3, 3), (1, 0), (3, 0), (0, 1), (0, 3),
)
PER_GROUP = NZ // GROUPS
GROUP_ROWS = PER_GROUP * ROWS
XY = NX * NY
NT = (((1,), (1,)), ((), ()))


def slot_of(offset):
    return Z_SLOTS.index(offset if offset != -8 else 8)


def device_at(dx, dy, dz, dc):
    wide = lax.axis_index("wide")
    grp = lax.axis_index("grp")
    x = (wide // 16 + dx) % NX
    y = ((wide // 4) % 4 + dy) % NY
    z = ((wide % 4) * 4 + grp // 2 + dz) % NZ
    core = (grp % 2 + dc) % NC
    return (x * 16 + y * 4 + z // 4, (z % 4) * 2 + core)


def remote(src, dst, send_sem, recv_sem, where):
    return pltpu.make_async_remote_copy(
        src_ref=src,
        dst_ref=dst,
        send_sem=send_sem,
        recv_sem=recv_sem,
        device_id=device_at(*where),
        device_id_type=MESH,
    )


def kernel(
    samples_hbm,
    archive_hbm,
    inv_hbm,
    mean_hbm,
    var_hbm,
    out_ref,
    own_raw,
    arch_raw,
    inv,
    coef,
    arch,
    arch_half,
    z_in,
    z_wide,
    main,
    part,
    part_own,
    xy_in,
    z_out,
    z_back,
    load_sem,
    swap_send,
    swap_recv,
    z_send,
    z_recv,
    one_send,
    one_recv,
    two_send,
    two_recv,
    xy_send,
    xy_recv,
    back_send,
    back_recv,
):
    z_partners = [(0, 0, d, 0) for d in NEAR]
    xy_partners = [(a, b, 0, 0) for a in range(NX) for b in range(NY) if a or b]
    partners = z_partners + xy_partners + [(0, 0, 0, 1)]
    barrier = pltpu.get_barrier_semaphore()
    for where in partners:
        pl.semaphore_signal(barrier, inc=1, device_id=device_at(*where), device_id_type=MESH)

    loads = [
        pltpu.make_async_copy(samples_hbm, own_raw, load_sem.at[0]),
        pltpu.make_async_copy(inv_hbm, inv, load_sem.at[1]),
        pltpu.make_async_copy(archive_hbm, arch_raw, load_sem.at[2]),
        pltpu.make_async_copy(mean_hbm, coef.at[0, pl.ds(0, OUT), pl.ds(0, RUNS)], load_sem.at[3]),
        pltpu.make_async_copy(var_hbm, coef.at[1, pl.ds(OUT, OUT), pl.ds(0, RUNS)], load_sem.at[4]),
    ]
    for load in loads:
        load.start()
    loads[0].wait()
    loads[1].wait()
    factor = inv[...] * DIN ** (-0.5)
    z_in[0] = (own_raw[...].astype(F32) * factor).astype(BF16)
    pl.semaphore_wait(barrier, len(partners))

    up, down, edge, far_up, far_down = [pl.ds(*span) for span in ((1, 4), (5, 3), (8, 1), (9, 4), (13, 3))]
    for offset in NEAR:
        there = slot_of(-offset)
        kind = 2 if there == 8 else 0 if there < 5 else 1
        remote(z_in.at[0], z_in.at[there], z_send.at[0], z_recv.at[kind], (0, 0, offset, 0)).start()
    loads[2].wait()
    scaled = (arch_raw[...].astype(F32) * factor).astype(BF16)
    arch[0:RUNS, :] = scaled
    wide_copy = scaled.astype(F32)
    half_norm = 0.5 * jnp.sum(wide_copy * wide_copy, axis=-1, keepdims=True)
    arch_half[:, 0:RUNS] = jnp.transpose(jnp.broadcast_to(half_norm, (RUNS, 128)))[0:8, :]
    loads[3].wait()
    loads[4].wait()
    coef[0, OUT : 2 * OUT, :] = jnp.zeros((OUT, 2 * RUNS), BF16)
    coef[1, 0:OUT, :] = jnp.zeros((OUT, 2 * RUNS), BF16)
    here, other = pl.ds(0, RUNS), pl.ds(RUNS, RUNS)
    low, high = pl.ds(0, OUT), pl.ds(OUT, OUT)
    swap = [
        remote(arch.at[here], arch.at[other], swap_send.at[0], swap_recv.at[0], (0, 0, 0, 1)),
        remote(arch_half.at[:, here], arch_half.at[:, other], swap_send.at[1], swap_recv.at[1], (0, 0, 0, 1)),
        remote(coef.at[0, low, here], coef.at[0, low, other], swap_send.at[2], swap_recv.at[2], (0, 0, 0, 1)),
        remote(coef.at[1, high, here], coef.at[1, high, other], swap_send.at[3], swap_recv.at[3], (0, 0, 0, 1)),
    ]
    for copy in swap:
        copy.start()

    rest = pl.ds(1, 3)

    def y_first(group):
        return group % 2 == 0

    def z_landed(span, kind):
        landed = z_in.at[span]
        remote(landed, landed, z_send.at[0], z_recv.at[kind], (0, 0, 1, 0)).wait_recv()

    def z_relay(span, target, kind, offset):
        remote(z_in.at[span], z_in.at[target], z_send.at[0], z_recv.at[kind], (0, 0, offset, 0)).start()

    def from_z(group):
        for place in range(PER_GROUP):
            z_wide[place * ROWS : (place + 1) * ROWS, :] = z_in[group * PER_GROUP + place].astype(F32)
        main[group, 0, 0] = z_wide[...].astype(BF16)
        if group in DIRECT:
            for a, b in FAR_STEPS:
                target = main.at[group, (4 - a) % 4, (4 - b) % 4]
                later = a if y_first(group) else b
                sends, receives = (two_send, two_recv) if later else (one_send, one_recv)
                remote(main.at[group, 0, 0], target, sends.at[group], receives.at[group], (a, b, 0, 0)).start()
            return
        for step in (1, 2, 3):
            back = 4 - step
            target = main.at[group, 0, back] if y_first(group) else main.at[group, back, 0]
            where = (0, step, 0, 0) if y_first(group) else (step, 0, 0, 0)
            remote(main.at[group, 0, 0], target, one_send.at[group], one_recv.at[group], where).start()

    def landed_one(group):
        return main.at[group, 0, rest] if y_first(group) else main.at[group, rest, 0]

    def landed_two(group):
        return main.at[group, rest] if y_first(group) else main.at[group, :, rest]

    def second(group):
        if group in DIRECT:
            return
        landed = landed_one(group)
        remote(landed, landed, one_send.at[group], one_recv.at[group], (1, 0, 0, 0)).wait_recv()
        for step in (1, 2, 3):
            back = 4 - step
            source = main.at[group, 0] if y_first(group) else main.at[group, :, 0]
            target = main.at[group, back] if y_first(group) else main.at[group, :, back]
            where = (step, 0, 0, 0) if y_first(group) else (0, step, 0, 0)
            remote(source, target, two_send.at[group], two_recv.at[group], where).start()

    def compute(group):
        landed = landed_two(group)
        if group in DIRECT:
            one = landed_one(group)
            remote(one, one, one_send.at[group], one_recv.at[group], (1, 0, 0, 0)).wait_recv()
        remote(landed, landed, two_send.at[group], two_recv.at[group], (1, 0, 0, 0)).wait_recv()
        block = main[group].reshape(XY * GROUP_ROWS, DIN)
        wide_block = block.astype(F32)
        samp_half = 0.5 * jnp.sum(wide_block * wide_block, axis=-1, keepdims=True)
        inner = lax.dot_general(block, arch[...], NT, preferred_element_type=F32)
        value = jnp.exp(inner - samp_half - arch_half[0:1, :])
        total = lax.dot_general(value.astype(BF16), coef[0], NT, preferred_element_type=F32)
        total = total + lax.dot_general((value * value).astype(BF16), coef[1], NT, preferred_element_type=F32)
        part_own[group] = total[0:GROUP_ROWS, :]
        part[group] = total.astype(BF16).reshape(XY, GROUP_ROWS, 2 * OUT)
        for a, b in FAR_STEPS:
            spot = a * NY + b
            there = ((NX - a) % NX) * NY + (NY - b) % NY
            remote(
                part.at[group, spot], xy_in.at[group, there], xy_send.at[group], xy_recv.at[group], (a, b, 0, 0)
            ).start()

    def reduce_xy(group):
        landed = xy_in.at[group, pl.ds(1, XY - 1)]
        remote(landed, landed, xy_send.at[group], xy_recv.at[group], (1, 0, 0, 0)).wait_recv()
        total = part_own[group] + jnp.sum(xy_in[group, 1:XY].astype(F32), axis=0)
        for place in range(PER_GROUP):
            slot = group * PER_GROUP + place
            z_out[slot] = total[place * ROWS : (place + 1) * ROWS, :]
            if slot:
                there = slot_of(-Z_SLOTS[slot])
                remote(
                    z_out.at[slot], z_back.at[there], back_send.at[0], back_recv.at[0], (0, 0, Z_SLOTS[slot], 0)
                ).start()

    z_landed(up, 0)
    z_relay(up, far_up, 3, -4)
    z_landed(down, 1)
    z_relay(down, far_down, 4, 4)
    from_z(0)
    from_z(1)
    second(0)
    second(1)
    z_landed(edge, 2)
    z_landed(far_up, 3)
    from_z(2)
    z_landed(far_down, 4)
    from_z(3)
    second(2)
    for copy in swap:
        copy.wait_recv()
    compute(0)
    compute(1)
    compute(2)
    compute(3)
    for group in range(GROUPS):
        reduce_xy(group)

    landed = z_back.at[pl.ds(1, NZ - 1)]
    remote(landed, landed, back_send.at[0], back_recv.at[0], (0, 0, 1, 0)).wait_recv()
    out_ref[...] = z_out[0] + jnp.sum(z_back[1:NZ], axis=0)

    sent = z_in.at[pl.ds(1, NZ - 1)]
    remote(sent, sent, z_send.at[0], z_recv.at[0], (0, 0, 1, 0)).wait_send()
    for copy in swap:
        copy.wait_send()
    for group in range(GROUPS):
        one, two, three = landed_one(group), landed_two(group), xy_in.at[group, pl.ds(1, XY - 1)]
        remote(one, one, one_send.at[group], one_recv.at[group], (1, 0, 0, 0)).wait_send()
        remote(two, two, two_send.at[group], two_recv.at[group], (1, 0, 0, 0)).wait_send()
        remote(three, three, xy_send.at[group], xy_recv.at[group], (1, 0, 0, 0)).wait_send()
    remote(landed, landed, back_send.at[0], back_recv.at[0], (0, 0, 1, 0)).wait_send()


def on_device(samples, archive, inv_len, mean_coef, var_coef):
    dma = pltpu.SemaphoreType.DMA
    sums = pl.pallas_call(
        kernel,
        out_shape=jax.ShapeDtypeStruct((ROWS, 2 * OUT), F32),
        in_specs=[pl.BlockSpec(memory_space=pl.ANY)] * 5,
        out_specs=pl.BlockSpec(memory_space=pltpu.VMEM),
        scratch_shapes=[
            pltpu.VMEM((ROWS, DIN), BF16),
            pltpu.VMEM((RUNS, DIN), BF16),
            pltpu.VMEM((1, DIN), F32),
            pltpu.VMEM((2, 2 * OUT, 2 * RUNS), BF16),
            pltpu.VMEM((2 * RUNS, DIN), BF16),
            pltpu.VMEM((8, 2 * RUNS), F32),
            pltpu.VMEM((NZ, ROWS, DIN), BF16),
            pltpu.VMEM((GROUP_ROWS, DIN), F32),
            pltpu.VMEM((GROUPS, NX, NY, GROUP_ROWS, DIN), BF16),
            pltpu.VMEM((GROUPS, XY, GROUP_ROWS, 2 * OUT), BF16),
            pltpu.VMEM((GROUPS, GROUP_ROWS, 2 * OUT), F32),
            pltpu.VMEM((GROUPS, XY, GROUP_ROWS, 2 * OUT), BF16),
            pltpu.VMEM((NZ, ROWS, 2 * OUT), F32),
            pltpu.VMEM((NZ, ROWS, 2 * OUT), F32),
            dma((5,)),
            dma((4,)),
            dma((4,)),
            dma((1,)),
            dma((5,)),
            dma((GROUPS,)),
            dma((GROUPS,)),
            dma((GROUPS,)),
            dma((GROUPS,)),
            dma((GROUPS,)),
            dma((GROUPS,)),
            dma((1,)),
            dma((1,)),
        ],
        name="surrogate",
        compiler_params=pltpu.CompilerParams(
            collective_id=0, has_side_effects=True, vmem_limit_bytes=32 << 20
        ),
    )(*[pltpu.with_memory_space_constraint(a, pltpu.HBM) for a in (samples, archive, inv_len.reshape(1, DIN), mean_coef.T, var_coef.T)])
    return (sums[:, :OUT], 1.0 - sums[:, OUT:])


def solution(mesh):
    rows = P(("wide", "grp"), None)
    return jax.shard_map(
        on_device,
        mesh=mesh,
        in_specs=(rows, rows, P(), rows, rows),
        out_specs=(rows, rows),
        check_vma=False,
    )
```

```python
import functools

import jax
import jax.numpy as jnp
from jax import lax
from jax.experimental import pallas as pl
from jax.experimental.pallas import tpu as pltpu
from jax.sharding import PartitionSpec as P

MESH = pl.DeviceIdType.MESH
F32 = jnp.float32
BF16 = jnp.bfloat16
DIN = 512
OUT = 64
ROWS = 4
RUNS = 512
NX, NY, NZ, NC = 4, 4, 16, 2
Z_SLOTS = (0, 1, 2, 3, 4, -1, -2, -3, -4, 5, 6, 7, 8, -5, -6, -7)
NEAR = (4, -4, 3, -3, 2, -2, 1, -1)
GROUPS = 4
LEAF, HUB = 0, 1
EXTRA = GROUPS
JOBS = GROUPS + 1
WORK = ((2, 0, 1), (2, 3, EXTRA, 0, 1))
DIRECT = (2, 3, EXTRA)
FAR_STEPS = (
    (2, 2), (2, 1), (2, 3), (1, 2), (3, 2), (2, 0), (0, 2), (1, 1),
    (1, 3), (3, 1), (3, 3), (1, 0), (3, 0), (0, 1), (0, 3),
)
PER_GROUP = NZ // GROUPS
GROUP_ROWS = PER_GROUP * ROWS
XY = NX * NY
NT = (((1,), (1,)), ((), ()))


def slot_of(offset):
    return Z_SLOTS.index(offset if offset != -8 else 8)


def device_at(dx, dy, dz, core):
    wide = lax.axis_index("wide")
    grp = lax.axis_index("grp")
    x = (wide // 16 + dx) % NX
    y = ((wide // 4) % 4 + dy) % NY
    z = ((wide % 4) * 4 + grp // 2 + dz) % NZ
    return (x * 16 + y * 4 + z // 4, (z % 4) * 2 + core)


def remote(src, dst, send_sem, recv_sem, where):
    return pltpu.make_async_remote_copy(
        src_ref=src,
        dst_ref=dst,
        send_sem=send_sem,
        recv_sem=recv_sem,
        device_id=device_at(*where),
        device_id_type=MESH,
    )


def kernel(
    samples_hbm,
    archive_hbm,
    inv_hbm,
    mean_hbm,
    var_hbm,
    out_ref,
    own_raw,
    own_z,
    arch_raw,
    inv,
    coef,
    arch,
    arch_half,
    z_in,
    z_wide,
    main,
    part,
    part_own,
    xy_in,
    z_out,
    z_back,
    load_sem,
    swap_send,
    swap_recv,
    z_send,
    z_recv,
    one_send,
    one_recv,
    two_send,
    two_recv,
    xy_send,
    xy_recv,
    back_send,
    back_recv,
):
    core = lax.axis_index("grp") % NC
    barrier = pltpu.get_barrier_semaphore()

    def partners_of(me):
        return [(0, 0, d, me) for d in NEAR] + [(a, b, 0, me) for a, b in FAR_STEPS] + [(0, 0, 0, 1 - me)]

    for me in (LEAF, HUB):

        @pl.when(core == me)
        def _():
            for where in partners_of(me):
                pl.semaphore_signal(barrier, inc=1, device_id=device_at(*where), device_id_type=MESH)

    loads = [
        pltpu.make_async_copy(samples_hbm, own_raw, load_sem.at[0]),
        pltpu.make_async_copy(inv_hbm, inv, load_sem.at[1]),
        pltpu.make_async_copy(archive_hbm, arch_raw, load_sem.at[2]),
        pltpu.make_async_copy(mean_hbm, coef.at[0, pl.ds(0, OUT), pl.ds(0, RUNS)], load_sem.at[3]),
        pltpu.make_async_copy(var_hbm, coef.at[1, pl.ds(OUT, OUT), pl.ds(0, RUNS)], load_sem.at[4]),
    ]
    for load in loads:
        load.start()
    loads[0].wait()
    loads[1].wait()
    factor = inv[...] * DIN ** (-0.5)
    own_z[...] = (own_raw[...].astype(F32) * factor).astype(BF16)
    up, down, edge, far_up, far_down = [pl.ds(*span) for span in ((1, 4), (5, 3), (8, 1), (9, 4), (13, 3))]
    up_most, last_up, far_most, last_far = pl.ds(1, 3), pl.ds(4, 1), pl.ds(9, 3), pl.ds(12, 1)

    def send_own(me):
        pl.semaphore_wait(barrier, len(partners_of(me)))
        for offset in NEAR:
            there = slot_of(-offset)
            kind = 2 if there == 8 else 0 if there < 5 else 1
            remote(own_z, z_in.at[there, me], z_send.at[0], z_recv.at[kind], (0, 0, offset, me)).start()
        z_in[0, me] = own_z[...]

    def prepare():
        loads[2].wait()
        scaled = (arch_raw[...].astype(F32) * factor).astype(BF16)
        arch[0:RUNS, :] = scaled
        wide_copy = scaled.astype(F32)
        half_norm = 0.5 * jnp.sum(wide_copy * wide_copy, axis=-1, keepdims=True)
        arch_half[:, 0:RUNS] = jnp.transpose(jnp.broadcast_to(half_norm, (RUNS, 128)))[0:8, :]
        loads[3].wait()
        loads[4].wait()
        coef[0, OUT : 2 * OUT, :] = jnp.zeros((OUT, 2 * RUNS), BF16)
        coef[1, 0:OUT, :] = jnp.zeros((OUT, 2 * RUNS), BF16)

    here, other = pl.ds(0, RUNS), pl.ds(RUNS, RUNS)
    low, high = pl.ds(0, OUT), pl.ds(OUT, OUT)

    def swap_of(me):
        where = (0, 0, 0, 1 - me)
        return [
            remote(arch.at[here], arch.at[other], swap_send.at[0], swap_recv.at[0], where),
            remote(arch_half.at[:, here], arch_half.at[:, other], swap_send.at[1], swap_recv.at[1], where),
            remote(coef.at[0, low, here], coef.at[0, low, other], swap_send.at[2], swap_recv.at[2], where),
            remote(coef.at[1, high, here], coef.at[1, high, other], swap_send.at[3], swap_recv.at[3], where),
        ]

    rest = pl.ds(1, 3)

    def y_first(group):
        return group % 2 == 0

    def z_landed(span, half, kind):
        landed = z_in.at[span, half]
        remote(landed, landed, z_send.at[0], z_recv.at[kind], (0, 0, 1, HUB)).wait_recv()

    def z_relay(span, target, half, kind, offset, core_there):
        remote(
            z_in.at[span, half], z_in.at[target, half], z_send.at[0], z_recv.at[kind], (0, 0, offset, core_there)
        ).start()

    def from_z(group, me):
        half, first = (LEAF, NZ - PER_GROUP) if group == EXTRA else (me, group * PER_GROUP)
        for place in range(PER_GROUP):
            z_wide[place * ROWS : (place + 1) * ROWS, :] = z_in[first + place, half].astype(F32)
        main[group, 0, 0] = z_wide[...].astype(BF16)
        for a, b in FAR_STEPS:
            later = a if y_first(group) else b
            if later and group not in DIRECT:
                continue
            target = main.at[group, (4 - a) % 4, (4 - b) % 4]
            sends, receives = (two_send, two_recv) if later else (one_send, one_recv)
            remote(main.at[group, 0, 0], target, sends.at[group], receives.at[group], (a, b, 0, me)).start()

    def landed_one(group):
        return main.at[group, 0, rest] if y_first(group) else main.at[group, rest, 0]

    def landed_two(group):
        return main.at[group, rest] if y_first(group) else main.at[group, :, rest]

    def second(group, me):
        landed = landed_one(group)
        remote(landed, landed, one_send.at[group], one_recv.at[group], (1, 0, 0, 0)).wait_recv()
        for step in (1, 2, 3):
            back = 4 - step
            source = main.at[group, 0] if y_first(group) else main.at[group, :, 0]
            target = main.at[group, back] if y_first(group) else main.at[group, :, back]
            where = (step, 0, 0, me) if y_first(group) else (0, step, 0, me)
            remote(source, target, two_send.at[group], two_recv.at[group], where).start()

    def compute(group, me):
        landed = landed_two(group)
        if group in DIRECT:
            one = landed_one(group)
            remote(one, one, one_send.at[group], one_recv.at[group], (1, 0, 0, 0)).wait_recv()
        remote(landed, landed, two_send.at[group], two_recv.at[group], (1, 0, 0, 0)).wait_recv()
        block = main[group].reshape(XY * GROUP_ROWS, DIN)
        wide_block = block.astype(F32)
        samp_half = 0.5 * jnp.sum(wide_block * wide_block, axis=-1, keepdims=True)
        inner = lax.dot_general(block, arch[...], NT, preferred_element_type=F32)
        value = jnp.exp(inner - samp_half - arch_half[0:1, :])
        total = lax.dot_general(value.astype(BF16), coef[0], NT, preferred_element_type=F32)
        total = total + lax.dot_general((value * value).astype(BF16), coef[1], NT, preferred_element_type=F32)
        part_own[group] = total[0:GROUP_ROWS, :]
        part[group] = total.astype(BF16).reshape(XY, GROUP_ROWS, 2 * OUT)
        for a, b in FAR_STEPS:
            spot = a * NY + b
            there = ((NX - a) % NX) * NY + (NY - b) % NY
            remote(
                part.at[group, spot], xy_in.at[group, there], xy_send.at[group], xy_recv.at[group], (a, b, 0, me)
            ).start()

    def reduce_xy(group, me):
        landed = xy_in.at[group, pl.ds(1, XY - 1)]
        remote(landed, landed, xy_send.at[group], xy_recv.at[group], (1, 0, 0, 0)).wait_recv()
        total = part_own[group] + jnp.sum(xy_in[group, 1:XY].astype(F32), axis=0)
        half, first = (LEAF, NZ - PER_GROUP) if group == EXTRA else (me, group * PER_GROUP)
        for place in range(PER_GROUP):
            slot = first + place
            piece = total[place * ROWS : (place + 1) * ROWS, :]
            if slot == 0:
                z_back[0] = piece
                continue
            leaving = group * PER_GROUP + place
            z_out[leaving] = piece
            remote(
                z_out.at[leaving],
                z_back.at[slot_of(-Z_SLOTS[slot])],
                back_send.at[0],
                back_recv.at[0],
                (0, 0, Z_SLOTS[slot], half),
            ).start()

    def run(me):
        jobs = WORK[me]
        send_own(me)
        prepare()
        swap = swap_of(me)
        for copy in swap:
            copy.start()
        z_landed(up, me, 0)
        if me == HUB:
            z_relay(up, far_up, me, 3, -4, HUB)
            z_landed(down, me, 1)
            z_relay(down, far_down, me, 4, 4, HUB)
            z_landed(edge, me, 2)
        else:
            z_relay(up_most, far_most, me, 3, -4, LEAF)
            z_landed(edge, me, 2)
            z_relay(last_up, last_far, me, 5, -4, HUB)
            z_landed(down, me, 1)
            z_relay(down, far_down, me, 6, 4, HUB)
        from_z(0, me)
        from_z(1, me)
        if me == HUB:
            z_landed(far_up, me, 3)
            from_z(2, me)
            z_landed(far_down, me, 4)
            from_z(3, me)
            z_landed(last_far, LEAF, 5)
            z_landed(far_down, LEAF, 6)
            from_z(EXTRA, me)
        else:
            z_landed(far_most, me, 3)
            from_z(2, me)
        second(0, me)
        second(1, me)
        for copy in swap:
            copy.wait_recv()
        for group in jobs:
            compute(group, me)
        for group in jobs:
            reduce_xy(group, me)
        landed = z_back.at[pl.ds(1, NZ - 1)]
        remote(landed, landed, back_send.at[0], back_recv.at[0], (0, 0, 1, me)).wait_recv()
        out_ref[...] = jnp.sum(z_back[...], axis=0)

        def drain(ref, sem):
            remote(ref, ref, sem, back_recv.at[0], (0, 0, 1, me)).wait_send()

        drain(z_in.at[pl.ds(1, NZ - 1), me], z_send.at[0])
        for copy in swap:
            copy.wait_send()
        for group in jobs:
            drain(landed_one(group), one_send.at[group])
            drain(landed_two(group), two_send.at[group])
            drain(xy_in.at[group, pl.ds(1, XY - 1)], xy_send.at[group])
        drain(z_out.at[pl.ds(1, len(jobs) * PER_GROUP - 1)], back_send.at[0])

    for me in (LEAF, HUB):

        @pl.when(core == me)
        def _():
            run(me)


def on_device(samples, archive, inv_len, mean_coef, var_coef):
    dma = pltpu.SemaphoreType.DMA
    sums = pl.pallas_call(
        kernel,
        out_shape=jax.ShapeDtypeStruct((ROWS, 2 * OUT), F32),
        in_specs=[pl.BlockSpec(memory_space=pl.ANY)] * 5,
        out_specs=pl.BlockSpec(memory_space=pltpu.VMEM),
        scratch_shapes=[
            pltpu.VMEM((ROWS, DIN), BF16),
            pltpu.VMEM((ROWS, DIN), BF16),
            pltpu.VMEM((RUNS, DIN), BF16),
            pltpu.VMEM((1, DIN), F32),
            pltpu.VMEM((2, 2 * OUT, 2 * RUNS), BF16),
            pltpu.VMEM((2 * RUNS, DIN), BF16),
            pltpu.VMEM((8, 2 * RUNS), F32),
            pltpu.VMEM((NZ, NC, ROWS, DIN), BF16),
            pltpu.VMEM((GROUP_ROWS, DIN), F32),
            pltpu.VMEM((JOBS, NX, NY, GROUP_ROWS, DIN), BF16),
            pltpu.VMEM((JOBS, XY, GROUP_ROWS, 2 * OUT), BF16),
            pltpu.VMEM((JOBS, GROUP_ROWS, 2 * OUT), F32),
            pltpu.VMEM((JOBS, XY, GROUP_ROWS, 2 * OUT), BF16),
            pltpu.VMEM((JOBS * PER_GROUP, ROWS, 2 * OUT), F32),
            pltpu.VMEM((NZ, ROWS, 2 * OUT), F32),
            dma((5,)),
            dma((4,)),
            dma((4,)),
            dma((1,)),
            dma((7,)),
            dma((JOBS,)),
            dma((JOBS,)),
            dma((JOBS,)),
            dma((JOBS,)),
            dma((JOBS,)),
            dma((JOBS,)),
            dma((1,)),
            dma((1,)),
        ],
        name="surrogate",
        compiler_params=pltpu.CompilerParams(
            collective_id=0, has_side_effects=True, vmem_limit_bytes=32 << 20
        ),
    )(*[pltpu.with_memory_space_constraint(a, pltpu.HBM) for a in (samples, archive, inv_len.reshape(1, DIN), mean_coef.T, var_coef.T)])
    return (sums[:, :OUT], 1.0 - sums[:, OUT:])


def solution(mesh):
    rows = P(("wide", "grp"), None)
    return jax.shard_map(
        on_device,
        mesh=mesh,
        in_specs=(rows, rows, P(), rows, rows),
        out_specs=(rows, rows),
        check_vma=False,
    )
```

```python
import functools

import jax
import jax.numpy as jnp
from jax import lax
from jax.experimental import pallas as pl
from jax.experimental.pallas import tpu as pltpu
from jax.sharding import PartitionSpec as P

MESH = pl.DeviceIdType.MESH
F32 = jnp.float32
BF16 = jnp.bfloat16
DIN = 512
OUT = 64
ROWS = 4
RUNS = 512
NX, NY, NZ, NC = 4, 4, 16, 2
Z_SLOTS = (0, 1, 2, 3, 4, -1, -2, -3, -4, 5, 6, 7, 8, -5, -6, -7)
NEAR = (4, -4, 3, -3, 2, -2, 1, -1)
GROUPS = 4
LEAF, HUB = 0, 1
EXTRA = GROUPS
JOBS = GROUPS + 1
WORK = ((2, 0, 1), (2, 3, EXTRA, 0, 1))
DIRECT = (2, 3, EXTRA)
FAR_STEPS = (
    (2, 2), (2, 1), (2, 3), (1, 2), (3, 2), (2, 0), (0, 2), (1, 1),
    (1, 3), (3, 1), (3, 3), (1, 0), (3, 0), (0, 1), (0, 3),
)
PER_GROUP = NZ // GROUPS
GROUP_ROWS = PER_GROUP * ROWS
XY = NX * NY
NT = (((1,), (1,)), ((), ()))


def slot_of(offset):
    return Z_SLOTS.index(offset if offset != -8 else 8)


def device_at(dx, dy, dz, core):
    wide = lax.axis_index("wide")
    grp = lax.axis_index("grp")
    x = (wide // 16 + dx) % NX
    y = ((wide // 4) % 4 + dy) % NY
    z = ((wide % 4) * 4 + grp // 2 + dz) % NZ
    return (x * 16 + y * 4 + z // 4, (z % 4) * 2 + core)


def remote(src, dst, send_sem, recv_sem, where):
    return pltpu.make_async_remote_copy(
        src_ref=src,
        dst_ref=dst,
        send_sem=send_sem,
        recv_sem=recv_sem,
        device_id=device_at(*where),
        device_id_type=MESH,
    )


def kernel(
    samples_hbm,
    archive_hbm,
    inv_hbm,
    mean_hbm,
    var_hbm,
    out_ref,
    own_raw,
    own_z,
    arch_raw,
    inv,
    coef,
    arch,
    arch_half,
    z_in,
    z_wide,
    main,
    part,
    part_own,
    xy_in,
    z_out,
    z_back,
    load_sem,
    swap_send,
    swap_recv,
    z_send,
    z_recv,
    one_send,
    one_recv,
    two_send,
    two_recv,
    xy_send,
    xy_recv,
    back_send,
    back_recv,
):
    core = lax.axis_index("grp") % NC
    barrier = pltpu.get_barrier_semaphore()

    def partners_of(me):
        plane = [(a, b, 0, me) for a, b in FAR_STEPS if a == 0 or b == 0]
        return [(0, 0, d, me) for d in NEAR] + plane + [(0, 0, 0, 1 - me)]

    for me in (LEAF, HUB):

        @pl.when(core == me)
        def _():
            for where in partners_of(me):
                pl.semaphore_signal(barrier, inc=1, device_id=device_at(*where), device_id_type=MESH)

    loads = [
        pltpu.make_async_copy(samples_hbm, own_raw, load_sem.at[0]),
        pltpu.make_async_copy(inv_hbm, inv, load_sem.at[1]),
        pltpu.make_async_copy(archive_hbm, arch_raw, load_sem.at[2]),
        pltpu.make_async_copy(mean_hbm, coef.at[0, pl.ds(0, OUT), pl.ds(0, RUNS)], load_sem.at[3]),
        pltpu.make_async_copy(var_hbm, coef.at[1, pl.ds(OUT, OUT), pl.ds(0, RUNS)], load_sem.at[4]),
    ]
    for load in loads:
        load.start()
    loads[0].wait()
    loads[1].wait()
    factor = inv[...] * DIN ** (-0.5)
    own_z[...] = (own_raw[...].astype(F32) * factor).astype(BF16)
    up, down, edge, far_up, far_down = [pl.ds(*span) for span in ((1, 4), (5, 3), (8, 1), (9, 4), (13, 3))]
    up_most, last_up, far_most, last_far = pl.ds(1, 3), pl.ds(4, 1), pl.ds(9, 3), pl.ds(12, 1)

    def send_own(me):
        pl.semaphore_wait(barrier, len(partners_of(me)))
        for offset in NEAR:
            there = slot_of(-offset)
            kind = 2 if there == 8 else 0 if there < 5 else 1
            remote(own_z, z_in.at[there, me], z_send.at[0], z_recv.at[kind], (0, 0, offset, me)).start()
        z_in[0, me] = own_z[...]

    def prepare():
        loads[2].wait()
        scaled = (arch_raw[...].astype(F32) * factor).astype(BF16)
        arch[0:RUNS, :] = scaled
        wide_copy = scaled.astype(F32)
        half_norm = 0.5 * jnp.sum(wide_copy * wide_copy, axis=-1, keepdims=True)
        arch_half[:, 0:RUNS] = jnp.transpose(jnp.broadcast_to(half_norm, (RUNS, 128)))[0:8, :]
        loads[3].wait()
        loads[4].wait()
        coef[0, OUT : 2 * OUT, :] = jnp.zeros((OUT, 2 * RUNS), BF16)
        coef[1, 0:OUT, :] = jnp.zeros((OUT, 2 * RUNS), BF16)

    here, other = pl.ds(0, RUNS), pl.ds(RUNS, RUNS)
    low, high = pl.ds(0, OUT), pl.ds(OUT, OUT)

    def swap_of(me):
        where = (0, 0, 0, 1 - me)
        return [
            remote(arch.at[here], arch.at[other], swap_send.at[0], swap_recv.at[0], where),
            remote(arch_half.at[:, here], arch_half.at[:, other], swap_send.at[1], swap_recv.at[1], where),
            remote(coef.at[0, low, here], coef.at[0, low, other], swap_send.at[2], swap_recv.at[2], where),
            remote(coef.at[1, high, here], coef.at[1, high, other], swap_send.at[3], swap_recv.at[3], where),
        ]

    rest = pl.ds(1, 3)

    def y_first(group):
        return group % 2 == 0

    def z_landed(span, half, kind):
        landed = z_in.at[span, half]
        remote(landed, landed, z_send.at[0], z_recv.at[kind], (0, 0, 1, HUB)).wait_recv()

    def z_relay(span, target, half, kind, offset, core_there):
        remote(
            z_in.at[span, half], z_in.at[target, half], z_send.at[0], z_recv.at[kind], (0, 0, offset, core_there)
        ).start()

    def from_z(group, me):
        half, first = (LEAF, NZ - PER_GROUP) if group == EXTRA else (me, group * PER_GROUP)
        for place in range(PER_GROUP):
            z_wide[place * ROWS : (place + 1) * ROWS, :] = z_in[first + place, half].astype(F32)
        main[group, 0, 0] = z_wide[...].astype(BF16)
        for a, b in FAR_STEPS:
            later = a if y_first(group) else b
            if later and group not in DIRECT:
                continue
            target = main.at[group, (4 - a) % 4, (4 - b) % 4]
            sends, receives = (two_send, two_recv) if later else (one_send, one_recv)
            remote(main.at[group, 0, 0], target, sends.at[group], receives.at[group], (a, b, 0, me)).start()

    def landed_one(group):
        return main.at[group, 0, rest] if y_first(group) else main.at[group, rest, 0]

    def landed_two(group):
        return main.at[group, rest] if y_first(group) else main.at[group, :, rest]

    def first_landed(group):
        landed = landed_one(group)
        remote(landed, landed, one_send.at[group], one_recv.at[group], (1, 0, 0, 0)).wait_recv()

    def second(group, me):
        for step in (1, 2, 3):
            back = 4 - step
            source = main.at[group, 0] if y_first(group) else main.at[group, :, 0]
            target = main.at[group, back] if y_first(group) else main.at[group, :, back]
            where = (step, 0, 0, me) if y_first(group) else (0, step, 0, me)
            remote(source, target, two_send.at[group], two_recv.at[group], where).start()

    def compute(group, me):
        landed = landed_two(group)
        if group in DIRECT:
            one = landed_one(group)
            remote(one, one, one_send.at[group], one_recv.at[group], (1, 0, 0, 0)).wait_recv()
        remote(landed, landed, two_send.at[group], two_recv.at[group], (1, 0, 0, 0)).wait_recv()
        block = main[group].reshape(XY * GROUP_ROWS, DIN)
        wide_block = block.astype(F32)
        samp_half = 0.5 * jnp.sum(wide_block * wide_block, axis=-1, keepdims=True)
        inner = lax.dot_general(block, arch[...], NT, preferred_element_type=F32)
        value = jnp.exp(inner - samp_half - arch_half[0:1, :])
        total = lax.dot_general(value.astype(BF16), coef[0], NT, preferred_element_type=F32)
        total = total + lax.dot_general((value * value).astype(BF16), coef[1], NT, preferred_element_type=F32)
        part_own[group] = total[0:GROUP_ROWS, :]
        part[group] = total.astype(BF16).reshape(XY, GROUP_ROWS, 2 * OUT)
        for a, b in FAR_STEPS:
            spot = a * NY + b
            there = ((NX - a) % NX) * NY + (NY - b) % NY
            remote(
                part.at[group, spot], xy_in.at[group, there], xy_send.at[group], xy_recv.at[group], (a, b, 0, me)
            ).start()

    def reduce_xy(group, me):
        landed = xy_in.at[group, pl.ds(1, XY - 1)]
        remote(landed, landed, xy_send.at[group], xy_recv.at[group], (1, 0, 0, 0)).wait_recv()
        total = part_own[group] + jnp.sum(xy_in[group, 1:XY].astype(F32), axis=0)
        half, first = (LEAF, NZ - PER_GROUP) if group == EXTRA else (me, group * PER_GROUP)
        for place in range(PER_GROUP):
            slot = first + place
            piece = total[place * ROWS : (place + 1) * ROWS, :]
            if slot == 0:
                z_back[0] = piece
                continue
            leaving = group * PER_GROUP + place
            z_out[leaving] = piece
            remote(
                z_out.at[leaving],
                z_back.at[slot_of(-Z_SLOTS[slot])],
                back_send.at[0],
                back_recv.at[0],
                (0, 0, Z_SLOTS[slot], half),
            ).start()

    def run(me):
        jobs = WORK[me]
        send_own(me)
        prepare()
        swap = swap_of(me)
        for copy in swap:
            copy.start()
        z_landed(up, me, 0)
        if me == HUB:
            z_relay(up, far_up, me, 3, -4, HUB)
            z_landed(down, me, 1)
            z_relay(down, far_down, me, 4, 4, HUB)
            z_landed(edge, me, 2)
        else:
            z_relay(up_most, far_most, me, 3, -4, LEAF)
            z_landed(edge, me, 2)
            z_relay(last_up, last_far, me, 5, -4, HUB)
            z_landed(down, me, 1)
            z_relay(down, far_down, me, 6, 4, HUB)
        from_z(0, me)
        from_z(1, me)
        first_landed(0)
        if me == HUB:
            z_landed(far_up, me, 3)
            from_z(2, me)
            z_landed(far_down, me, 4)
            from_z(3, me)
            z_landed(last_far, LEAF, 5)
            z_landed(far_down, LEAF, 6)
            from_z(EXTRA, me)
        else:
            z_landed(far_most, me, 3)
            from_z(2, me)
        second(0, me)
        first_landed(1)
        second(1, me)
        for copy in swap:
            copy.wait_recv()
        for group in jobs:
            compute(group, me)
        for group in jobs:
            reduce_xy(group, me)
        landed = z_back.at[pl.ds(1, NZ - 1)]
        remote(landed, landed, back_send.at[0], back_recv.at[0], (0, 0, 1, me)).wait_recv()
        out_ref[...] = jnp.sum(z_back[...], axis=0)

        def drain(ref, sem):
            remote(ref, ref, sem, back_recv.at[0], (0, 0, 1, me)).wait_send()

        drain(z_in.at[pl.ds(1, NZ - 1), me], z_send.at[0])
        for copy in swap:
            copy.wait_send()
        for group in jobs:
            drain(landed_one(group), one_send.at[group])
            drain(landed_two(group), two_send.at[group])
            drain(xy_in.at[group, pl.ds(1, XY - 1)], xy_send.at[group])
        drain(z_out.at[pl.ds(1, len(jobs) * PER_GROUP - 1)], back_send.at[0])

    for me in (LEAF, HUB):

        @pl.when(core == me)
        def _():
            run(me)


def on_device(samples, archive, inv_len, mean_coef, var_coef):
    dma = pltpu.SemaphoreType.DMA
    sums = pl.pallas_call(
        kernel,
        out_shape=jax.ShapeDtypeStruct((ROWS, 2 * OUT), F32),
        in_specs=[pl.BlockSpec(memory_space=pl.ANY)] * 5,
        out_specs=pl.BlockSpec(memory_space=pltpu.VMEM),
        scratch_shapes=[
            pltpu.VMEM((ROWS, DIN), BF16),
            pltpu.VMEM((ROWS, DIN), BF16),
            pltpu.VMEM((RUNS, DIN), BF16),
            pltpu.VMEM((1, DIN), F32),
            pltpu.VMEM((2, 2 * OUT, 2 * RUNS), BF16),
            pltpu.VMEM((2 * RUNS, DIN), BF16),
            pltpu.VMEM((8, 2 * RUNS), F32),
            pltpu.VMEM((NZ, NC, ROWS, DIN), BF16),
            pltpu.VMEM((GROUP_ROWS, DIN), F32),
            pltpu.VMEM((JOBS, NX, NY, GROUP_ROWS, DIN), BF16),
            pltpu.VMEM((JOBS, XY, GROUP_ROWS, 2 * OUT), BF16),
            pltpu.VMEM((JOBS, GROUP_ROWS, 2 * OUT), F32),
            pltpu.VMEM((JOBS, XY, GROUP_ROWS, 2 * OUT), BF16),
            pltpu.VMEM((JOBS * PER_GROUP, ROWS, 2 * OUT), F32),
            pltpu.VMEM((NZ, ROWS, 2 * OUT), F32),
            dma((5,)),
            dma((4,)),
            dma((4,)),
            dma((1,)),
            dma((7,)),
            dma((JOBS,)),
            dma((JOBS,)),
            dma((JOBS,)),
            dma((JOBS,)),
            dma((JOBS,)),
            dma((JOBS,)),
            dma((1,)),
            dma((1,)),
        ],
        name="surrogate",
        compiler_params=pltpu.CompilerParams(
            collective_id=0, has_side_effects=True, vmem_limit_bytes=32 << 20
        ),
    )(*[pltpu.with_memory_space_constraint(a, pltpu.HBM) for a in (samples, archive, inv_len.reshape(1, DIN), mean_coef.T, var_coef.T)])
    return (sums[:, :OUT], 1.0 - sums[:, OUT:])


def solution(mesh):
    rows = P(("wide", "grp"), None)
    return jax.shard_map(
        on_device,
        mesh=mesh,
        in_specs=(rows, rows, P(), rows, rows),
        out_specs=(rows, rows),
        check_vma=False,
    )
```

```python
import functools

import jax
import jax.numpy as jnp
from jax import lax
from jax.experimental import pallas as pl
from jax.experimental.pallas import tpu as pltpu
from jax.sharding import PartitionSpec as P

MESH = pl.DeviceIdType.MESH
F32 = jnp.float32
BF16 = jnp.bfloat16
DIN = 512
OUT = 64
ROWS = 4
RUNS = 512
NX, NY, NZ, NC = 4, 4, 16, 2
Z_SLOTS = (0, 1, 2, 3, 4, -1, -2, -3, -4, 5, 6, 7, 8, -5, -6, -7)
NEAR = (4, -4, 3, -3, 2, -2, 1, -1)
GROUPS = 4
LEAF, HUB = 0, 1
EXTRA = GROUPS
JOBS = GROUPS + 1
WORK = ((2, 0, 1), (2, 3, EXTRA, 0, 1))
DIRECT = (2, 3, EXTRA)
FAR_STEPS = (
    (2, 2), (2, 1), (2, 3), (1, 2), (3, 2), (2, 0), (0, 2), (1, 1),
    (1, 3), (3, 1), (3, 3), (1, 0), (3, 0), (0, 1), (0, 3),
)
PER_GROUP = NZ // GROUPS
GROUP_ROWS = PER_GROUP * ROWS
XY = NX * NY
NT = (((1,), (1,)), ((), ()))


def slot_of(offset):
    return Z_SLOTS.index(offset if offset != -8 else 8)


def device_at(dx, dy, dz, core):
    wide = lax.axis_index("wide")
    grp = lax.axis_index("grp")
    x = (wide // 16 + dx) % NX
    y = ((wide // 4) % 4 + dy) % NY
    z = ((wide % 4) * 4 + grp // 2 + dz) % NZ
    return (x * 16 + y * 4 + z // 4, (z % 4) * 2 + core)


def remote(src, dst, send_sem, recv_sem, where):
    return pltpu.make_async_remote_copy(
        src_ref=src,
        dst_ref=dst,
        send_sem=send_sem,
        recv_sem=recv_sem,
        device_id=device_at(*where),
        device_id_type=MESH,
    )


def kernel(
    samples_hbm,
    archive_hbm,
    inv_hbm,
    mean_hbm,
    var_hbm,
    out_ref,
    own_raw,
    own_z,
    arch_raw,
    inv,
    coef,
    arch,
    arch_half,
    z_in,
    z_wide,
    main,
    part,
    part_own,
    xy_in,
    z_out,
    z_back,
    load_sem,
    swap_send,
    swap_recv,
    z_send,
    z_recv,
    one_send,
    one_recv,
    two_send,
    two_recv,
    xy_send,
    xy_recv,
    back_send,
    back_recv,
):
    core = lax.axis_index("grp") % NC
    barrier = pltpu.get_barrier_semaphore()

    def partners_of(me):
        return [(0, 0, d, me) for d in NEAR] + [(a, b, 0, me) for a, b in FAR_STEPS] + [(0, 0, 0, 1 - me)]

    for me in (LEAF, HUB):

        @pl.when(core == me)
        def _():
            for where in partners_of(me):
                pl.semaphore_signal(barrier, inc=1, device_id=device_at(*where), device_id_type=MESH)

    loads = [
        pltpu.make_async_copy(samples_hbm, own_raw, load_sem.at[0]),
        pltpu.make_async_copy(inv_hbm, inv, load_sem.at[1]),
        pltpu.make_async_copy(archive_hbm, arch_raw, load_sem.at[2]),
        pltpu.make_async_copy(mean_hbm, coef.at[0, pl.ds(0, OUT), pl.ds(0, RUNS)], load_sem.at[3]),
        pltpu.make_async_copy(var_hbm, coef.at[1, pl.ds(OUT, OUT), pl.ds(0, RUNS)], load_sem.at[4]),
    ]
    for load in loads:
        load.start()
    loads[0].wait()
    loads[1].wait()
    factor = inv[...] * DIN ** (-0.5)
    own_z[...] = (own_raw[...].astype(F32) * factor).astype(BF16)
    up, down, edge, far_up, far_down = [pl.ds(*span) for span in ((1, 4), (5, 3), (8, 1), (9, 4), (13, 3))]
    up_most, last_up, far_most, last_far = pl.ds(1, 3), pl.ds(4, 1), pl.ds(9, 3), pl.ds(12, 1)

    def send_own(me):
        pl.semaphore_wait(barrier, len(partners_of(me)))
        for offset in NEAR:
            there = slot_of(-offset)
            kind = 2 if there == 8 else 0 if there < 5 else 1
            remote(own_z, z_in.at[there, me], z_send.at[0], z_recv.at[kind], (0, 0, offset, me)).start()
        z_in[0, me] = own_z[...]

    def prepare():
        loads[2].wait()
        scaled = (arch_raw[...].astype(F32) * factor).astype(BF16)
        arch[0:RUNS, :] = scaled
        wide_copy = scaled.astype(F32)
        half_norm = 0.5 * jnp.sum(wide_copy * wide_copy, axis=-1, keepdims=True)
        arch_half[:, 0:RUNS] = jnp.transpose(jnp.broadcast_to(half_norm, (RUNS, 128)))[0:8, :]
        loads[3].wait()
        loads[4].wait()
        coef[0, OUT : 2 * OUT, :] = jnp.zeros((OUT, 2 * RUNS), BF16)
        coef[1, 0:OUT, :] = jnp.zeros((OUT, 2 * RUNS), BF16)

    here, other = pl.ds(0, RUNS), pl.ds(RUNS, RUNS)
    low, high = pl.ds(0, OUT), pl.ds(OUT, OUT)

    def swap_of(me):
        where = (0, 0, 0, 1 - me)
        return [
            remote(arch.at[here], arch.at[other], swap_send.at[0], swap_recv.at[0], where),
            remote(arch_half.at[:, here], arch_half.at[:, other], swap_send.at[1], swap_recv.at[1], where),
            remote(coef.at[0, low, here], coef.at[0, low, other], swap_send.at[2], swap_recv.at[2], where),
            remote(coef.at[1, high, here], coef.at[1, high, other], swap_send.at[3], swap_recv.at[3], where),
        ]

    rest = pl.ds(1, 3)

    def y_first(group):
        return group % 2 == 0

    def z_landed(span, half, kind):
        landed = z_in.at[span, half]
        remote(landed, landed, z_send.at[0], z_recv.at[kind], (0, 0, 1, HUB)).wait_recv()

    def z_relay(span, target, half, kind, offset, core_there):
        remote(
            z_in.at[span, half], z_in.at[target, half], z_send.at[0], z_recv.at[kind], (0, 0, offset, core_there)
        ).start()

    def from_z(group, me):
        half, first = (LEAF, NZ - PER_GROUP) if group == EXTRA else (me, group * PER_GROUP)
        for place in range(PER_GROUP):
            z_wide[place * ROWS : (place + 1) * ROWS, :] = z_in[first + place, half].astype(F32)
        main[group, 0, 0] = z_wide[...].astype(BF16)
        for a, b in FAR_STEPS:
            later = a if y_first(group) else b
            if later and group not in DIRECT:
                continue
            target = main.at[group, (4 - a) % 4, (4 - b) % 4]
            sends, receives = (two_send, two_recv) if later else (one_send, one_recv)
            remote(main.at[group, 0, 0], target, sends.at[group], receives.at[group], (a, b, 0, me)).start()

    def landed_one(group):
        return main.at[group, 0, rest] if y_first(group) else main.at[group, rest, 0]

    def landed_two(group):
        return main.at[group, rest] if y_first(group) else main.at[group, :, rest]

    def second(group, me):
        landed = landed_one(group)
        remote(landed, landed, one_send.at[group], one_recv.at[group], (1, 0, 0, 0)).wait_recv()
        for step in (1, 2, 3):
            back = 4 - step
            source = main.at[group, 0] if y_first(group) else main.at[group, :, 0]
            target = main.at[group, back] if y_first(group) else main.at[group, :, back]
            where = (step, 0, 0, me) if y_first(group) else (0, step, 0, me)
            remote(source, target, two_send.at[group], two_recv.at[group], where).start()

    def compute(group, me):
        landed = landed_two(group)
        if group in DIRECT:
            one = landed_one(group)
            remote(one, one, one_send.at[group], one_recv.at[group], (1, 0, 0, 0)).wait_recv()
        remote(landed, landed, two_send.at[group], two_recv.at[group], (1, 0, 0, 0)).wait_recv()
        block = main[group].reshape(XY * GROUP_ROWS, DIN)
        wide_block = block.astype(F32)
        samp_half = 0.5 * jnp.sum(wide_block * wide_block, axis=-1, keepdims=True)
        inner = lax.dot_general(block, arch[...], NT, preferred_element_type=F32)
        value = jnp.exp(inner - samp_half - arch_half[0:1, :])
        total = lax.dot_general(value.astype(BF16), coef[0], NT, preferred_element_type=F32)
        total = total + lax.dot_general((value * value).astype(BF16), coef[1], NT, preferred_element_type=F32)
        part_own[group] = total[0:GROUP_ROWS, :]
        part[group] = total.astype(BF16).reshape(XY, GROUP_ROWS, 2 * OUT)
        for a, b in FAR_STEPS:
            spot = a * NY + b
            there = ((NX - a) % NX) * NY + (NY - b) % NY
            remote(
                part.at[group, spot], xy_in.at[group, there], xy_send.at[group], xy_recv.at[group], (a, b, 0, me)
            ).start()

    def reduce_xy(group, me):
        landed = xy_in.at[group, pl.ds(1, XY - 1)]
        remote(landed, landed, xy_send.at[group], xy_recv.at[group], (1, 0, 0, 0)).wait_recv()
        total = part_own[group] + jnp.sum(xy_in[group, 1:XY].astype(F32), axis=0)
        half, first = (LEAF, NZ - PER_GROUP) if group == EXTRA else (me, group * PER_GROUP)
        for place in range(PER_GROUP):
            slot = first + place
            piece = total[place * ROWS : (place + 1) * ROWS, :]
            if slot == 0:
                z_back[0] = piece
                continue
            leaving = group * PER_GROUP + place
            z_out[leaving] = piece
            remote(
                z_out.at[leaving],
                z_back.at[slot_of(-Z_SLOTS[slot])],
                back_send.at[0],
                back_recv.at[0],
                (0, 0, Z_SLOTS[slot], half),
            ).start()

    def run(me):
        jobs = WORK[me]
        send_own(me)
        prepare()
        swap = swap_of(me)
        for copy in swap:
            copy.start()
        z_landed(up, me, 0)
        if me == HUB:
            z_relay(up, far_up, me, 3, -4, HUB)
            z_landed(down, me, 1)
            z_relay(down, far_down, me, 4, 4, HUB)
            z_landed(edge, me, 2)
        else:
            z_relay(up_most, far_most, me, 3, -4, LEAF)
            z_landed(edge, me, 2)
            z_relay(last_up, last_far, me, 5, -4, HUB)
            z_landed(down, me, 1)
            z_relay(down, far_down, me, 6, 4, HUB)
        from_z(0, me)
        from_z(1, me)
        if me == HUB:
            z_landed(far_up, me, 3)
            from_z(2, me)
            z_landed(far_down, me, 4)
            from_z(3, me)
            z_landed(last_far, LEAF, 5)
            z_landed(far_down, LEAF, 6)
            from_z(EXTRA, me)
        else:
            z_landed(far_most, me, 3)
            from_z(2, me)
        if me == LEAF:
            second(0, me)
            second(1, me)
        for copy in swap:
            copy.wait_recv()
        for group in jobs:
            compute(group, me)
            if group == 2 and me == HUB:
                second(0, me)
                second(1, me)
        for group in jobs:
            reduce_xy(group, me)
        landed = z_back.at[pl.ds(1, NZ - 1)]
        remote(landed, landed, back_send.at[0], back_recv.at[0], (0, 0, 1, me)).wait_recv()
        out_ref[...] = jnp.sum(z_back[...], axis=0)

        def drain(ref, sem):
            remote(ref, ref, sem, back_recv.at[0], (0, 0, 1, me)).wait_send()

        drain(z_in.at[pl.ds(1, NZ - 1), me], z_send.at[0])
        for copy in swap:
            copy.wait_send()
        for group in jobs:
            drain(landed_one(group), one_send.at[group])
            drain(landed_two(group), two_send.at[group])
            drain(xy_in.at[group, pl.ds(1, XY - 1)], xy_send.at[group])
        drain(z_out.at[pl.ds(1, len(jobs) * PER_GROUP - 1)], back_send.at[0])

    for me in (LEAF, HUB):

        @pl.when(core == me)
        def _():
            run(me)


def on_device(samples, archive, inv_len, mean_coef, var_coef):
    dma = pltpu.SemaphoreType.DMA
    sums = pl.pallas_call(
        kernel,
        out_shape=jax.ShapeDtypeStruct((ROWS, 2 * OUT), F32),
        in_specs=[pl.BlockSpec(memory_space=pl.ANY)] * 5,
        out_specs=pl.BlockSpec(memory_space=pltpu.VMEM),
        scratch_shapes=[
            pltpu.VMEM((ROWS, DIN), BF16),
            pltpu.VMEM((ROWS, DIN), BF16),
            pltpu.VMEM((RUNS, DIN), BF16),
            pltpu.VMEM((1, DIN), F32),
            pltpu.VMEM((2, 2 * OUT, 2 * RUNS), BF16),
            pltpu.VMEM((2 * RUNS, DIN), BF16),
            pltpu.VMEM((8, 2 * RUNS), F32),
            pltpu.VMEM((NZ, NC, ROWS, DIN), BF16),
            pltpu.VMEM((GROUP_ROWS, DIN), F32),
            pltpu.VMEM((JOBS, NX, NY, GROUP_ROWS, DIN), BF16),
            pltpu.VMEM((JOBS, XY, GROUP_ROWS, 2 * OUT), BF16),
            pltpu.VMEM((JOBS, GROUP_ROWS, 2 * OUT), F32),
            pltpu.VMEM((JOBS, XY, GROUP_ROWS, 2 * OUT), BF16),
            pltpu.VMEM((JOBS * PER_GROUP, ROWS, 2 * OUT), F32),
            pltpu.VMEM((NZ, ROWS, 2 * OUT), F32),
            dma((5,)),
            dma((4,)),
            dma((4,)),
            dma((1,)),
            dma((7,)),
            dma((JOBS,)),
            dma((JOBS,)),
            dma((JOBS,)),
            dma((JOBS,)),
            dma((JOBS,)),
            dma((JOBS,)),
            dma((1,)),
            dma((1,)),
        ],
        name="surrogate",
        compiler_params=pltpu.CompilerParams(
            collective_id=0, has_side_effects=True, vmem_limit_bytes=32 << 20
        ),
    )(*[pltpu.with_memory_space_constraint(a, pltpu.HBM) for a in (samples, archive, inv_len.reshape(1, DIN), mean_coef.T, var_coef.T)])
    return (sums[:, :OUT], 1.0 - sums[:, OUT:])


def solution(mesh):
    rows = P(("wide", "grp"), None)
    return jax.shard_map(
        on_device,
        mesh=mesh,
        in_specs=(rows, rows, P(), rows, rows),
        out_specs=(rows, rows),
        check_vma=False,
    )
```
